256 devices in a mesh: prefix: 8 (over z), feat: 32 (over y, x, core).
Axes of the slice: x: 4, y: 4, z: 8, core: 2. Of those that a mesh axis runs over, the one named last changes fastest.
Arguments:
- activations: float32 [1024, 1152], P('feat'), may hold values from -6 to 6
- enc_weight: float32 [16, 9216, 1152], P('prefix', 'feat'), may hold values from -0.1875 to 0.1875
- dec_weight: float32 [16, 9216, 1152], P('prefix', 'feat'), may hold values from -0.0625 to 0.0625
Outputs:
- enc_grad: float32 [16, 9216, 1152], P('prefix', 'feat')
- dec_grad: float32 [16, 9216, 1152], P('prefix', 'feat')
The draws below stay inside these ranges and needn't reach their ends.
All inputs are finite; a program needn't handle non-finite values.
Results may differ from the reference program's by a relative error of at most 0.000094.
Values sent between devices are 32-bit elements; how exact they have to be, the bound alone decides.
No kernel may reach another device: no remote copies, remote signals or barrier semaphores. Data moves between devices by JAX's collectives and lax.ppermute only.
A program may use at most 128 MiB of HBM per device.

```python
import jax
import jax.numpy as jnp
from jax import lax

D = 1152
GROUPS = 16
FPG = 9216
TOK = 1024


def block_levels(stream_key, extent, cuts, low, largest):
    factor_of, own = 1.0, jax.random.fold_in(stream_key, 6)
    for dim, shards_of in cuts:
        heights = jnp.exp(jax.random.uniform(jax.random.fold_in(own, dim), (shards_of,), jnp.float32, low / len(cuts), largest / len(cuts)))
        factor_of = factor_of * jnp.repeat(heights, extent[dim] // shards_of).reshape([-1 if axis == dim else 1 for axis in range(len(extent))])
    return factor_of


def noise(stream_key, extent, scale, limit, split=(), held_as=jnp.bfloat16):
    drawn = scale * jax.random.normal(stream_key, extent, jnp.float32)
    if split:
        drawn = drawn * block_levels(stream_key, extent, split, -0.22, 0.18)
    return jnp.clip(drawn, -limit, limit).astype(held_as)


def setup_inputs(seed: int = 0) -> dict:
    seeds = jax.random.split(jax.random.key(seed), 4)
    activations = noise(seeds[0], (TOK, D), 1.0, 6.0, ((0, 32),), jnp.float32)
    enc_weight = noise(seeds[1], (GROUPS, FPG, D), D ** -0.5, 0.1875, ((0, 8), (1, 32)), jnp.float32)
    dec_weight = noise(seeds[2], (GROUPS, FPG, D), FPG ** -0.5, 0.0625, ((0, 8), (1, 32)), jnp.float32)
    return dict(activations=activations, enc_weight=enc_weight, dec_weight=dec_weight)


HIGHEST = lax.Precision.HIGHEST


def reference(activations, enc_weight, dec_weight):
    def decode_group(weights):
        enc_rows, dec_rows = weights
        pre_act = jnp.dot(activations, enc_rows.T, precision=HIGHEST)
        features = jax.nn.softplus(4.0 * pre_act) / 4.0
        return jnp.dot(features, dec_rows, precision=HIGHEST)

    decoded = lax.map(decode_group, (enc_weight, dec_weight))
    rebuilt = jnp.cumsum(decoded, axis=0)
    errors = rebuilt - activations[None, :, :]
    suffix = (2.0 / TOK) * jnp.flip(jnp.cumsum(jnp.flip(errors, 0), axis=0), 0)

    def gradients(triple):
        enc_rows, dec_rows, suffix_rows = triple
        pre_act = jnp.dot(activations, enc_rows.T, precision=HIGHEST)
        features = jax.nn.softplus(4.0 * pre_act) / 4.0
        slopes = jax.nn.sigmoid(4.0 * pre_act)
        dec_part = jnp.dot(features.T, suffix_rows, precision=HIGHEST)
        gate = jnp.dot(suffix_rows, dec_rows.T, precision=HIGHEST) * slopes
        enc_part = jnp.dot(gate.T, activations, precision=HIGHEST)
        return enc_part, dec_part

    enc_grad, dec_grad = lax.map(gradients, (enc_weight, dec_weight, suffix))
    return (enc_grad, dec_grad)
```

```python
import jax
import jax.numpy as jnp
from jax import lax
from jax.sharding import PartitionSpec as P

HIGH = lax.Precision.HIGH
CHUNKS = 2


def feat_index(y, x, core):
    return (y % 4) * 8 + (x % 4) * 2 + core


def from_chip(value, axis, step):
    dy, dx = (step, 0) if axis == 0 else (0, step)
    pairs = [
        (feat_index(y + dy, x + dx, c), feat_index(y, x, c))
        for y in range(4)
        for x in range(4)
        for c in range(2)
    ]
    return lax.ppermute(value, "feat", pairs)


def from_other_core(value):
    return lax.ppermute(value, "feat", [(f, f ^ 1) for f in range(32)])


def gather_line(value, axis):
    return [value] + [from_chip(value, axis, e) for e in (1, 2, 3)]


def scatter_line(pieces, axis):
    total = pieces[0]
    for e in (1, 3, 2):
        total = total + from_chip(pieces[(-e) % 4], axis, e)
    return total


def suffix_sums(decoded, act, factor):
    count = decoded.shape[0]
    errors = []
    total = decoded[0]
    for m in range(count):
        if m:
            total = total + decoded[m]
        errors.append(total - act)
    out = [None] * count
    run = errors[count - 1]
    out[count - 1] = run
    for m in range(count - 2, -1, -1):
        run = run + errors[m]
        out[m] = run
    return factor * jnp.stack(out)


def per_device(activations, enc_weight, dec_weight):
    rows, width = activations.shape
    groups, feats, _ = enc_weight.shape
    tokens = rows * lax.axis_size("feat")
    zs = lax.axis_size("prefix")
    factor = 2.0 / tokens
    part = rows // CHUNKS
    own = part // zs
    enc_all = jnp.concatenate([enc_weight, from_other_core(enc_weight)], axis=1)
    dec_all = jnp.concatenate([dec_weight, from_other_core(dec_weight)], axis=1)
    firsts = [1, 0]
    chunks = []
    for k in range(CHUNKS):
        first, second = firsts[k], 1 - firsts[k]
        act = activations[k * part : (k + 1) * part]
        line = jnp.stack(gather_line(act, second))
        chunks.append(jnp.stack(gather_line(line, first)).reshape(-1, width))
    feat_k, slope_k, totals = [], [], []
    for k in range(CHUNKS):
        first, second = firsts[k], 1 - firsts[k]
        pre = jnp.einsum("gkd,nd->gkn", enc_all, chunks[k], precision=HIGH)
        features = jax.nn.softplus(4.0 * pre) / 4.0
        feat_k.append(features)
        slope_k.append(jax.nn.sigmoid(4.0 * pre))
        made = jnp.einsum("gkn,gkd->gnd", features, dec_all, precision=HIGH)
        made = made.reshape(groups, 4, 4, part, width)
        line = scatter_line([made[:, e] for e in range(4)], first)
        totals.append(scatter_line([line[:, e] for e in range(4)], second))
    sent = jnp.stack(totals).reshape(CHUNKS, groups, zs, own, width)
    sent = sent.transpose(2, 1, 0, 3, 4).reshape(zs, groups * CHUNKS * own, width)
    got = lax.all_to_all(sent, "prefix", 0, 0)
    decoded = got.reshape(zs * groups, CHUNKS * own, width)
    here = lax.axis_index("prefix")
    act = activations.reshape(CHUNKS, zs, own, width)
    act = lax.dynamic_index_in_dim(act, here, 1, keepdims=False)
    suffix = suffix_sums(decoded, act.reshape(CHUNKS * own, width), factor)
    back = lax.all_to_all(suffix.reshape(zs, groups * CHUNKS * own, width), "prefix", 0, 0)
    back = back.reshape(zs, groups, CHUNKS, own, width).transpose(2, 1, 0, 3, 4)
    back = back.reshape(CHUNKS, groups, part, width)
    dec_new = 0.0
    enc_new = 0.0
    for k in range(CHUNKS):
        first, second = firsts[k], 1 - firsts[k]
        line = jnp.stack(gather_line(back[k], second), axis=1)
        plane = jnp.stack(gather_line(line, first), axis=1)
        suf = plane.reshape(groups, -1, width)
        gate = jnp.einsum("gkd,gnd->gkn", dec_all, suf, precision=HIGH) * slope_k[k]
        dec_new = dec_new + jnp.einsum("gkn,gnd->gkd", feat_k[k], suf, precision=HIGH)
        enc_new = enc_new + jnp.einsum("gkn,nd->gkd", gate, chunks[k], precision=HIGH)
    dec_new = dec_new[:, :feats] + from_other_core(dec_new[:, feats:])
    enc_new = enc_new[:, :feats] + from_other_core(enc_new[:, feats:])
    return (enc_new, dec_new)


def solution(mesh):
    in_specs = (P("feat", None), P("prefix", "feat", None), P("prefix", "feat", None))
    out_specs = (P("prefix", "feat", None), P("prefix", "feat", None))
    return jax.shard_map(
        per_device, mesh=mesh, in_specs=in_specs, out_specs=out_specs, check_vma=False
    )
```

```python
import functools

import jax
import jax.numpy as jnp
from jax import lax
from jax.experimental import pallas as pl
from jax.experimental.pallas import tpu as pltpu
from jax.sharding import PartitionSpec as P


F32 = jnp.float32
HIGH = lax.Precision.HIGH


def feat_index(y, x, core):
    return (y % 4) * 8 + (x % 4) * 2 + core


def from_chip(value, axis, step):
    dy, dx = (step, 0) if axis == 0 else (0, step)
    pairs = [
        (feat_index(y + dy, x + dx, c), feat_index(y, x, c))
        for y in range(4)
        for x in range(4)
        for c in range(2)
    ]
    return lax.ppermute(value, "feat", pairs)


def from_other_core(value):
    return lax.ppermute(value, "feat", [(f, f ^ 1) for f in range(32)])


def pack_kernel(*refs):
    out = refs[8]
    zs = out.shape[0]
    for k in range(2):
        for g in range(2):
            total = refs[4 * k][g]
            for r in refs[4 * k + 1 : 4 * k + 4]:
                total = total + r[g]
            own = total.shape[0] // zs
            at = (2 * g + k) * own
            for z in range(zs):
                out[z, at : at + own] = total[z * own : (z + 1) * own]


def unpack_kernel(back, a, b):
    zs = back.shape[0]
    own = a.shape[1] // zs
    for k, ref in enumerate((a, b)):
        for g in range(2):
            at = (2 * g + k) * own
            for z in range(zs):
                ref[g, z * own : (z + 1) * own] = back[z, at : at + own]


def suffix_kernel(factor, got, act, out):
    zs, rows, _ = got.shape
    half = rows // 2
    a = act[...]
    errors = []
    total = None
    for z in range(zs):
        for g in range(2):
            d = got[z, g * half : (g + 1) * half]
            total = d if total is None else total + d
            errors.append(total - a)
    run = None
    for m in range(2 * zs - 1, -1, -1):
        run = errors[m] if run is None else run + errors[m]
        z, g = m // 2, m % 2
        out[z, g * half : (g + 1) * half] = factor * run


def shape(*dims, dtype=F32):
    return jax.ShapeDtypeStruct(dims, dtype)


def flat_call(body, ins, outs):
    vmem = pl.BlockSpec(memory_space=pltpu.VMEM)
    return pl.pallas_call(
        body, in_specs=[vmem] * len(ins), out_specs=[vmem] * len(outs), out_shape=outs
    )(*ins)


def step(activations, enc_weight, dec_weight):
    rows, width = activations.shape
    groups, feats, _ = enc_weight.shape
    tokens = rows * lax.axis_size("feat")
    zs = lax.axis_size("prefix")
    factor = 2.0 / tokens
    part = rows // 2
    own = part // zs
    n = 4 * part
    dots = functools.partial(jnp.einsum, precision=HIGH)
    acts = [activations[:part], activations[part:]]
    halves = range(2)

    lines = []
    for k in halves:
        got = [acts[k]] + [from_chip(acts[k], k, e) for e in (1, 2, 3)]
        lines.append(jnp.concatenate(got, axis=0))
    x = {(0, k): lines[k] for k in halves}
    for e in (1, 3, 2):
        for k in halves:
            x[e, k] = from_chip(lines[k], 1 - k, e)

    enc_all = jnp.concatenate([enc_weight, from_other_core(enc_weight)], axis=1)
    dec_all = jnp.concatenate([dec_weight, from_other_core(dec_weight)], axis=1)
    pairs = ((1, 3), (2, 0))
    keys = [[(e, k) for e in pair for k in halves] for pair in pairs]
    feat_p, made, xs = [], {}, []
    for p in range(2):
        xs.append(jnp.concatenate([x[key] for key in keys[p]], axis=0))
        pre = dots("gkd,nd->gkn", enc_all, xs[p])
        feat_p.append(jax.nn.softplus(4.0 * pre) / 4.0)
        out = dots("gkn,gkd->gnd", feat_p[p], dec_all)
        for i, key in enumerate(keys[p]):
            made[key] = out[:, i * n : (i + 1) * n]
        if p:
            late = (made[2, 0], made[2, 1], out)
            made[2, 0], made[2, 1], out = lax.optimization_barrier(late)
            for k in halves:
                made[0, k] = out[:, (2 + k) * n : (3 + k) * n]

    moved = {}
    for e in (1, 3, 2):
        for k in halves:
            moved[e, k] = from_chip(made[e, k], 1 - k, (-e) % 4)
    terms = []
    for k in halves:
        line = made[0, k] + moved[1, k] + moved[3, k]
        line = lax.optimization_barrier(line) + moved[2, k]
        line = line.reshape(groups, 4, part, width)
        terms.append(line[:, 0])
        for e in (1, 3, 2):
            terms.append(from_chip(line[:, e], k, (-e) % 4))
    (sent,) = flat_call(pack_kernel, terms, [shape(zs, 4 * own, width)])
    act = activations.reshape(2, zs, own, width)
    act = lax.dynamic_index_in_dim(act, lax.axis_index("prefix"), 1, keepdims=False)
    sent, act = lax.optimization_barrier((sent, act.reshape(2 * own, width)))
    got = lax.all_to_all(sent, "prefix", 0, 0)
    (suffix,) = flat_call(
        functools.partial(suffix_kernel, factor),
        (got, act),
        [shape(zs, 4 * own, width)],
    )
    back = lax.all_to_all(suffix, "prefix", 0, 0)
    mine = flat_call(unpack_kernel, (back,), [shape(groups, part, width)] * 2)

    s = {}
    for k in halves:
        got = [mine[k]] + [from_chip(mine[k], k, e) for e in (1, 2, 3)]
        s[0, k] = jnp.concatenate(got, axis=1)
    for e in (1, 3, 2):
        for k in halves:
            s[e, k] = from_chip(s[0, k], 1 - k, e)

    sums = {}
    for p in range(2):
        suf = jnp.concatenate([s[key] for key in keys[p]], axis=1)
        for at in (1, 0):
            of = slice(at * feats, (at + 1) * feats)
            features = feat_p[p][:, of]
            slopes = -jnp.expm1(-4.0 * features)
            gate = dots("gkd,gnd->gkn", dec_all[:, of], suf) * slopes
            enc = dots("gkn,nd->gkd", gate, xs[p])
            dec = dots("gkn,gnd->gkd", features, suf)
            if p:
                enc, dec = enc + sums["enc", at], dec + sums["dec", at]
            sums["enc", at], sums["dec", at] = enc, dec
    enc_new = sums["enc", 0] + from_other_core(sums["enc", 1])
    dec_new = sums["dec", 0] + from_other_core(sums["dec", 1])
    return (enc_new, dec_new)


def solution(mesh):
    in_specs = (P("feat", None), P("prefix", "feat", None), P("prefix", "feat", None))
    out_specs = (P("prefix", "feat", None), P("prefix", "feat", None))
    return jax.shard_map(
        step, mesh=mesh, in_specs=in_specs, out_specs=out_specs, check_vma=False
    )
```

```python
import functools

import jax
import jax.numpy as jnp
from jax import lax
from jax.experimental import pallas as pl
from jax.experimental.pallas import tpu as pltpu
from jax.sharding import PartitionSpec as P


F32 = jnp.float32
HIGH = lax.Precision.HIGH


def feat_index(y, x, core):
    return (y % 4) * 8 + (x % 4) * 2 + core


def from_chip(value, axis, step):
    dy, dx = (step, 0) if axis == 0 else (0, step)
    pairs = [
        (feat_index(y + dy, x + dx, c), feat_index(y, x, c))
        for y in range(4)
        for x in range(4)
        for c in range(2)
    ]
    return lax.ppermute(value, "feat", pairs)


def from_other_core(value):
    return lax.ppermute(value, "feat", [(f, f ^ 1) for f in range(32)])


def pack_kernel(*refs):
    out = refs[8]
    zs = out.shape[0]
    for k in range(2):
        for g in range(2):
            total = refs[4 * k][g]
            for r in refs[4 * k + 1 : 4 * k + 4]:
                total = total + r[g]
            own = total.shape[0] // zs
            at = (2 * g + k) * own
            for z in range(zs):
                out[z, at : at + own] = total[z * own : (z + 1) * own]


def unpack_kernel(back, a, b):
    zs = back.shape[0]
    own = a.shape[1] // zs
    for k, ref in enumerate((a, b)):
        for g in range(2):
            at = (2 * g + k) * own
            for z in range(zs):
                ref[g, z * own : (z + 1) * own] = back[z, at : at + own]


def suffix_kernel(factor, got, act, out):
    zs, rows, _ = got.shape
    half = rows // 2
    a = act[...]
    errors = []
    total = None
    for z in range(zs):
        for g in range(2):
            d = got[z, g * half : (g + 1) * half]
            total = d if total is None else total + d
            errors.append(total - a)
    run = None
    for m in range(2 * zs - 1, -1, -1):
        run = errors[m] if run is None else run + errors[m]
        z, g = m // 2, m % 2
        out[z, g * half : (g + 1) * half] = factor * run


def shape(*dims, dtype=F32):
    return jax.ShapeDtypeStruct(dims, dtype)


def flat_call(body, ins, outs):
    vmem = pl.BlockSpec(memory_space=pltpu.VMEM)
    return pl.pallas_call(
        body,
        in_specs=[vmem] * len(ins),
        out_specs=[vmem] * len(outs),
        out_shape=outs,
        compiler_params=pltpu.CompilerParams(vmem_limit_bytes=4 * 2**20),
    )(*ins)


def join_kernel(eo, ep, do, dp, ea, da):
    half = eo.shape[1]
    for own, other, both in ((eo, ep, ea), (do, dp, da)):
        both[0, :half] = own[0]
        both[0, half:] = other[0]


def join(enc_own, enc_other, dec_own, dec_other):
    groups, feats, width = enc_own.shape
    part = pl.BlockSpec((1, feats, width), lambda g: (g, 0, 0))
    both = pl.BlockSpec((1, 2 * feats, width), lambda g: (g, 0, 0))
    return pl.pallas_call(
        join_kernel,
        name="join",
        grid=(groups,),
        in_specs=[part] * 4,
        out_specs=[both] * 2,
        out_shape=[shape(groups, 2 * feats, width)] * 2,
        compiler_params=pltpu.CompilerParams(vmem_limit_bytes=24 * 2**20),
    )(enc_own, enc_other, dec_own, dec_other)


def step(activations, enc_weight, dec_weight):
    rows, width = activations.shape
    groups, feats, _ = enc_weight.shape
    tokens = rows * lax.axis_size("feat")
    zs = lax.axis_size("prefix")
    factor = 2.0 / tokens
    part = rows // 2
    own = part // zs
    n = 4 * part
    dots = functools.partial(jnp.einsum, precision=HIGH)
    acts = [activations[:part], activations[part:]]
    halves = range(2)

    lines = []
    for k in halves:
        got = [acts[k]] + [from_chip(acts[k], k, e) for e in (1, 2, 3)]
        lines.append(jnp.concatenate(got, axis=0))
    x = {(0, k): lines[k] for k in halves}
    for e in (1, 3, 2):
        for k in halves:
            x[e, k] = from_chip(lines[k], 1 - k, e)

    enc_other, dec_other = from_other_core(enc_weight), from_other_core(dec_weight)
    enc_all, dec_all = join(enc_weight, enc_other, dec_weight, dec_other)
    dec_of = (dec_weight, dec_other)
    pairs = ((1, 3), (2, 0))
    keys = [[(e, k) for e in pair for k in halves] for pair in pairs]
    feat_p, made, xs = [], {}, []
    for p in range(2):
        xs.append(jnp.concatenate([x[key] for key in keys[p]], axis=0))
        pre = dots("gkd,nd->gkn", enc_all, xs[p])
        feat_p.append(jax.nn.softplus(4.0 * pre) / 4.0)
        if p == 0:
            out = dots("gkn,gkd->gnd", feat_p[p], dec_all)
            for i, key in enumerate(keys[p]):
                made[key] = out[:, i * n : (i + 1) * n]
            continue
        far = dots("gkn,gkd->gnd", feat_p[p][:, :, : 2 * n], dec_all)
        near = dots("gkn,gkd->gnd", feat_p[p][:, :, 2 * n :], dec_all)
        for k in halves:
            made[2, k] = far[:, k * n : (k + 1) * n]
            made[0, k] = near[:, k * n : (k + 1) * n]

    moved = {}
    for e in (1, 3, 2):
        for k in halves:
            moved[e, k] = from_chip(made[e, k], 1 - k, (-e) % 4)
    terms = []
    for k in halves:
        line = made[0, k] + moved[1, k] + moved[3, k]
        line = lax.optimization_barrier(line) + moved[2, k]
        line = line.reshape(groups, 4, part, width)
        terms.append(line[:, 0])
        for e in (1, 3, 2):
            terms.append(from_chip(line[:, e], k, (-e) % 4))
    (sent,) = flat_call(pack_kernel, terms, [shape(zs, 4 * own, width)])
    act = activations.reshape(2, zs, own, width)
    act = lax.dynamic_index_in_dim(act, lax.axis_index("prefix"), 1, keepdims=False)
    sent, act = lax.optimization_barrier((sent, act.reshape(2 * own, width)))
    got = lax.all_to_all(sent, "prefix", 0, 0)
    (suffix,) = flat_call(
        functools.partial(suffix_kernel, factor),
        (got, act),
        [shape(zs, 4 * own, width)],
    )
    back = lax.all_to_all(suffix, "prefix", 0, 0)
    mine = flat_call(unpack_kernel, (back,), [shape(groups, part, width)] * 2)

    s = {}
    for k in halves:
        got = [mine[k]] + [from_chip(mine[k], k, e) for e in (1, 2, 3)]
        s[0, k] = jnp.concatenate(got, axis=1)
    for e in (1, 3, 2):
        for k in halves:
            s[e, k] = from_chip(s[0, k], 1 - k, e)

    sums = {}
    for p in range(2):
        suf = jnp.concatenate([s[key] for key in keys[p]], axis=1)
        for at in (1, 0):
            of = slice(at * feats, (at + 1) * feats)
            features = feat_p[p][:, of]
            slopes = -jnp.expm1(-4.0 * features)
            gate = dots("gkd,gnd->gkn", dec_of[at], suf) * slopes
            enc = dots("gkn,nd->gkd", gate, xs[p])
            dec = dots("gkn,gnd->gkd", features, suf)
            if p:
                enc, dec = enc + sums["enc", at], dec + sums["dec", at]
            sums["enc", at], sums["dec", at] = enc, dec
    enc_new = sums["enc", 0] + from_other_core(sums["enc", 1])
    dec_new = sums["dec", 0] + from_other_core(sums["dec", 1])
    return (enc_new, dec_new)


def solution(mesh):
    in_specs = (P("feat", None), P("prefix", "feat", None), P("prefix", "feat", None))
    out_specs = (P("prefix", "feat", None), P("prefix", "feat", None))
    return jax.shard_map(
        step, mesh=mesh, in_specs=in_specs, out_specs=out_specs, check_vma=False
    )
```

```python
import functools

import jax
import jax.numpy as jnp
from jax import lax
from jax.experimental import pallas as pl
from jax.experimental.pallas import tpu as pltpu
from jax.sharding import PartitionSpec as P


F32 = jnp.float32
HIGH = lax.Precision.HIGH


def feat_index(y, x, core):
    return (y % 4) * 8 + (x % 4) * 2 + core


def from_chip(value, axis, step):
    dy, dx = (step, 0) if axis == 0 else (0, step)
    pairs = [
        (feat_index(y + dy, x + dx, c), feat_index(y, x, c))
        for y in range(4)
        for x in range(4)
        for c in range(2)
    ]
    return lax.ppermute(value, "feat", pairs)


def from_other_core(value):
    return lax.ppermute(value, "feat", [(f, f ^ 1) for f in range(32)])


def pack_kernel(*refs):
    out = refs[8]
    zs = out.shape[0]
    for k in range(2):
        for g in range(2):
            total = refs[4 * k][g]
            for r in refs[4 * k + 1 : 4 * k + 4]:
                total = total + r[g]
            own = total.shape[0] // zs
            at = (2 * g + k) * own
            for z in range(zs):
                out[z, at : at + own] = total[z * own : (z + 1) * own]


def unpack_kernel(back, a, b):
    zs = back.shape[0]
    own = a.shape[1] // zs
    for k, ref in enumerate((a, b)):
        for g in range(2):
            at = (2 * g + k) * own
            for z in range(zs):
                ref[g, z * own : (z + 1) * own] = back[z, at : at + own]


def suffix_kernel(factor, here, got, act, out):
    zs, rows, _ = got.shape
    half = rows // 2
    own = half // 2
    part = act.shape[0] // 2
    picked = []
    for k in range(2):
        a = act[k * part : k * part + own]
        for z in range(1, zs):
            at = k * part + z * own
            a = jnp.where(here[0] == z, act[at : at + own], a)
        picked.append(a)
    a = jnp.concatenate(picked, axis=0)
    errors = []
    total = None
    for z in range(zs):
        for g in range(2):
            d = got[z, g * half : (g + 1) * half]
            total = d if total is None else total + d
            errors.append(total - a)
    run = None
    for m in range(2 * zs - 1, -1, -1):
        run = errors[m] if run is None else run + errors[m]
        z, g = m // 2, m % 2
        out[z, g * half : (g + 1) * half] = factor * run


def shape(*dims, dtype=F32):
    return jax.ShapeDtypeStruct(dims, dtype)


def flat_call(body, ins, outs):
    vmem = pl.BlockSpec(memory_space=pltpu.VMEM)
    return pl.pallas_call(
        body,
        in_specs=[vmem] * len(ins),
        out_specs=[vmem] * len(outs),
        out_shape=outs,
        compiler_params=pltpu.CompilerParams(vmem_limit_bytes=4 * 2**20),
    )(*ins)


def join_kernel(eo, ep, do, dp, ea, da):
    half = eo.shape[1]
    for own, other, both in ((eo, ep, ea), (do, dp, da)):
        both[0, :half] = own[0]
        both[0, half:] = other[0]


def join(enc_own, enc_other, dec_own, dec_other):
    groups, feats, width = enc_own.shape
    part = pl.BlockSpec((1, feats, width), lambda g: (g, 0, 0))
    both = pl.BlockSpec((1, 2 * feats, width), lambda g: (g, 0, 0))
    return pl.pallas_call(
        join_kernel,
        name="join",
        grid=(groups,),
        in_specs=[part] * 4,
        out_specs=[both] * 2,
        out_shape=[shape(groups, 2 * feats, width)] * 2,
        compiler_params=pltpu.CompilerParams(vmem_limit_bytes=24 * 2**20),
    )(enc_own, enc_other, dec_own, dec_other)


def step(activations, enc_weight, dec_weight):
    rows, width = activations.shape
    groups, feats, _ = enc_weight.shape
    tokens = rows * lax.axis_size("feat")
    zs = lax.axis_size("prefix")
    factor = 2.0 / tokens
    part = rows // 2
    own = part // zs
    n = 4 * part
    dots = functools.partial(jnp.einsum, precision=HIGH)
    acts = [activations[:part], activations[part:]]
    halves = range(2)

    lines = []
    for k in halves:
        got = [acts[k]] + [from_chip(acts[k], k, e) for e in (1, 2, 3)]
        lines.append(jnp.concatenate(got, axis=0))
    x = {(0, k): lines[k] for k in halves}
    for e in (1, 3, 2):
        for k in halves:
            x[e, k] = from_chip(lines[k], 1 - k, e)

    enc_other, dec_other = from_other_core(enc_weight), from_other_core(dec_weight)
    enc_all, dec_all = join(enc_weight, enc_other, dec_weight, dec_other)
    dec_of = (dec_weight, dec_other)
    pairs = ((1, 3), (2, 0))
    keys = [[(e, k) for e in pair for k in halves] for pair in pairs]
    feat_p, made, xs = [], {}, []
    for p in range(2):
        xs.append(jnp.concatenate([x[key] for key in keys[p]], axis=0))
        pre = dots("gkd,nd->gkn", enc_all, xs[p])
        feat_p.append(jax.nn.softplus(4.0 * pre) / 4.0)
        if p == 0:
            out = dots("gkn,gkd->gnd", feat_p[p], dec_all)
            for i, key in enumerate(keys[p]):
                made[key] = out[:, i * n : (i + 1) * n]
            continue
        far = dots("gkn,gkd->gnd", feat_p[p][:, :, : 2 * n], dec_all)
        near = dots("gkn,gkd->gnd", feat_p[p][:, :, 2 * n :], dec_all)
        for k in halves:
            made[2, k] = far[:, k * n : (k + 1) * n]
            made[0, k] = near[:, k * n : (k + 1) * n]

    moved = {}
    for e in (1, 3, 2):
        for k in halves:
            moved[e, k] = from_chip(made[e, k], 1 - k, (-e) % 4)
    terms = []
    for k in halves:
        line = made[0, k] + moved[1, k] + moved[3, k]
        line = lax.optimization_barrier(line) + moved[2, k]
        line = line.reshape(groups, 4, part, width)
        terms.append(line[:, 0])
        for e in (1, 3, 2):
            terms.append(from_chip(line[:, e], k, (-e) % 4))
    (sent,) = flat_call(pack_kernel, terms, [shape(zs, 4 * own, width)])
    here = lax.axis_index("prefix").reshape(1)
    sent, here = lax.optimization_barrier((sent, here))
    got = lax.all_to_all(sent, "prefix", 0, 0)
    vmem = pl.BlockSpec(memory_space=pltpu.VMEM)
    suffix = pl.pallas_call(
        functools.partial(suffix_kernel, factor),
        name="suffix",
        in_specs=[pl.BlockSpec(memory_space=pltpu.SMEM), vmem, vmem],
        out_specs=vmem,
        out_shape=shape(zs, 4 * own, width),
        compiler_params=pltpu.CompilerParams(vmem_limit_bytes=4 * 2**20),
    )(here, got, activations)
    back = lax.all_to_all(suffix, "prefix", 0, 0)
    mine = flat_call(unpack_kernel, (back,), [shape(groups, part, width)] * 2)

    s = {}
    for k in halves:
        got = [mine[k]] + [from_chip(mine[k], k, e) for e in (1, 2, 3)]
        s[0, k] = jnp.concatenate(got, axis=1)
    for e in (1, 3, 2):
        for k in halves:
            s[e, k] = from_chip(s[0, k], 1 - k, e)

    sums = {}
    for p in range(2):
        suf = jnp.concatenate([s[key] for key in keys[p]], axis=1)
        for at in (1, 0):
            of = slice(at * feats, (at + 1) * feats)
            features = feat_p[p][:, of]
            slopes = -jnp.expm1(-4.0 * features)
            gate = dots("gkd,gnd->gkn", dec_of[at], suf) * slopes
            enc = dots("gkn,nd->gkd", gate, xs[p])
            dec = dots("gkn,gnd->gkd", features, suf)
            if p:
                enc, dec = enc + sums["enc", at], dec + sums["dec", at]
            sums["enc", at], sums["dec", at] = enc, dec
    enc_new = sums["enc", 0] + from_other_core(sums["enc", 1])
    dec_new = sums["dec", 0] + from_other_core(sums["dec", 1])
    return (enc_new, dec_new)


def solution(mesh):
    in_specs = (P("feat", None), P("prefix", "feat", None), P("prefix", "feat", None))
    out_specs = (P("prefix", "feat", None), P("prefix", "feat", None))
    return jax.shard_map(
        step, mesh=mesh, in_specs=in_specs, out_specs=out_specs, check_vma=False
    )
```

```python
import functools

import jax
import jax.numpy as jnp
from jax import lax
from jax.experimental import pallas as pl
from jax.experimental.pallas import tpu as pltpu
from jax.sharding import PartitionSpec as P


F32 = jnp.float32
HIGH = lax.Precision.HIGH


def feat_index(y, x, core):
    return (y % 4) * 8 + (x % 4) * 2 + core


def from_chip(value, axis, step):
    dy, dx = (step, 0) if axis == 0 else (0, step)
    pairs = [
        (feat_index(y + dy, x + dx, c), feat_index(y, x, c))
        for y in range(4)
        for x in range(4)
        for c in range(2)
    ]
    return lax.ppermute(value, "feat", pairs)


def from_other_core(value):
    return lax.ppermute(value, "feat", [(f, f ^ 1) for f in range(32)])


def pack_kernel(*refs):
    out = refs[8]
    zs = out.shape[0]
    for k in range(2):
        for g in range(2):
            total = refs[4 * k][g]
            for r in refs[4 * k + 1 : 4 * k + 4]:
                total = total + r[g]
            own = total.shape[0] // zs
            at = (2 * g + k) * own
            for z in range(zs):
                out[z, at : at + own] = total[z * own : (z + 1) * own]


def unpack_kernel(back, a, b):
    zs = back.shape[0]
    own = a.shape[1] // zs
    for k, ref in enumerate((a, b)):
        for g in range(2):
            at = (2 * g + k) * own
            for z in range(zs):
                ref[g, z * own : (z + 1) * own] = back[z, at : at + own]


def suffix_kernel(factor, here, got, act, out):
    zs, rows, _ = got.shape
    half = rows // 2
    own = half // 2
    part = act.shape[0] // 2
    picked = []
    for k in range(2):
        a = act[k * part : k * part + own]
        for z in range(1, zs):
            at = k * part + z * own
            a = jnp.where(here[0] == z, act[at : at + own], a)
        picked.append(a)
    a = jnp.concatenate(picked, axis=0)
    errors = []
    total = None
    for z in range(zs):
        for g in range(2):
            d = got[z, g * half : (g + 1) * half]
            total = d if total is None else total + d
            errors.append(total - a)
    run = None
    for m in range(2 * zs - 1, -1, -1):
        run = errors[m] if run is None else run + errors[m]
        z, g = m // 2, m % 2
        out[z, g * half : (g + 1) * half] = factor * run


def shape(*dims, dtype=F32):
    return jax.ShapeDtypeStruct(dims, dtype)


def flat_call(body, ins, outs):
    vmem = pl.BlockSpec(memory_space=pltpu.VMEM)
    return pl.pallas_call(
        body,
        in_specs=[vmem] * len(ins),
        out_specs=[vmem] * len(outs),
        out_shape=outs,
        compiler_params=pltpu.CompilerParams(vmem_limit_bytes=4 * 2**20),
    )(*ins)


def line_kernel(*refs):
    out = refs[4]
    for i, r in enumerate(refs[:4]):
        rows = r.shape[1]
        out[:, i * rows : (i + 1) * rows] = r[...]


def join_kernel(eo, ep, do, dp, ea, da):
    half = eo.shape[1]
    for own, other, both in ((eo, ep, ea), (do, dp, da)):
        both[0, :half] = own[0]
        both[0, half:] = other[0]


def join(enc_own, enc_other, dec_own, dec_other):
    groups, feats, width = enc_own.shape
    part = pl.BlockSpec((1, feats, width), lambda g: (g, 0, 0))
    both = pl.BlockSpec((1, 2 * feats, width), lambda g: (g, 0, 0))
    return pl.pallas_call(
        join_kernel,
        name="join",
        grid=(groups,),
        in_specs=[part] * 4,
        out_specs=[both] * 2,
        out_shape=[shape(groups, 2 * feats, width)] * 2,
        compiler_params=pltpu.CompilerParams(vmem_limit_bytes=24 * 2**20),
    )(enc_own, enc_other, dec_own, dec_other)


def step(activations, enc_weight, dec_weight):
    rows, width = activations.shape
    groups, feats, _ = enc_weight.shape
    tokens = rows * lax.axis_size("feat")
    zs = lax.axis_size("prefix")
    factor = 2.0 / tokens
    part = rows // 2
    own = part // zs
    n = 4 * part
    dots = functools.partial(jnp.einsum, precision=HIGH)
    acts = [activations[:part], activations[part:]]
    halves = range(2)

    lines = []
    for k in halves:
        got = [acts[k]] + [from_chip(acts[k], k, e) for e in (1, 2, 3)]
        lines.append(jnp.concatenate(got, axis=0))
    x = {(0, k): lines[k] for k in halves}
    for e in (1, 3, 2):
        for k in halves:
            x[e, k] = from_chip(lines[k], 1 - k, e)

    enc_other, dec_other = from_other_core(enc_weight), from_other_core(dec_weight)
    enc_all, dec_all = join(enc_weight, enc_other, dec_weight, dec_other)
    dec_of = (dec_weight, dec_other)
    pairs = ((1, 3), (2, 0))
    keys = [[(e, k) for e in pair for k in halves] for pair in pairs]
    feat_p, made, xs = [], {}, []
    for p in range(2):
        xs.append(jnp.concatenate([x[key] for key in keys[p]], axis=0))
        pre = dots("gkd,nd->gkn", enc_all, xs[p])
        feat_p.append(jax.nn.softplus(4.0 * pre) / 4.0)
        if p == 0:
            out = dots("gkn,gkd->gnd", feat_p[p], dec_all)
            for i, key in enumerate(keys[p]):
                made[key] = out[:, i * n : (i + 1) * n]
            continue
        far = dots("gkn,gkd->gnd", feat_p[p][:, :, : 2 * n], dec_all)
        near = dots("gkn,gkd->gnd", feat_p[p][:, :, 2 * n :], dec_all)
        for k in halves:
            made[2, k] = far[:, k * n : (k + 1) * n]
            made[0, k] = near[:, k * n : (k + 1) * n]

    moved = {}
    for e in (1, 3, 2):
        for k in halves:
            moved[e, k] = from_chip(made[e, k], 1 - k, (-e) % 4)
    terms = []
    for k in halves:
        line = made[0, k] + moved[1, k] + moved[3, k]
        line = lax.optimization_barrier(line) + moved[2, k]
        line = line.reshape(groups, 4, part, width)
        terms.append(line[:, 0])
        for e in (1, 3, 2):
            terms.append(from_chip(line[:, e], k, (-e) % 4))
    (sent,) = flat_call(pack_kernel, terms, [shape(zs, 4 * own, width)])
    here = lax.axis_index("prefix").reshape(1)
    sent, here = lax.optimization_barrier((sent, here))
    got = lax.all_to_all(sent, "prefix", 0, 0)
    vmem = pl.BlockSpec(memory_space=pltpu.VMEM)
    suffix = pl.pallas_call(
        functools.partial(suffix_kernel, factor),
        name="suffix",
        in_specs=[pl.BlockSpec(memory_space=pltpu.SMEM), vmem, vmem],
        out_specs=vmem,
        out_shape=shape(zs, 4 * own, width),
        compiler_params=pltpu.CompilerParams(vmem_limit_bytes=4 * 2**20),
    )(here, got, activations)
    back = lax.all_to_all(suffix, "prefix", 0, 0)
    mine = flat_call(unpack_kernel, (back,), [shape(groups, part, width)] * 2)

    s = {}
    for k in halves:
        got = [mine[k]] + [from_chip(mine[k], k, e) for e in (1, 2, 3)]
        (s[0, k],) = flat_call(line_kernel, got, [shape(groups, n, width)])
    for e in (1, 3, 2):
        for k in halves:
            s[e, k] = from_chip(s[0, k], 1 - k, e)

    sums = {}
    for p in range(2):
        suf = jnp.concatenate([s[key] for key in keys[p]], axis=1)
        for at in (1, 0):
            of = slice(at * feats, (at + 1) * feats)
            features = feat_p[p][:, of]
            slopes = -jnp.expm1(-4.0 * features)
            gate = dots("gkd,gnd->gkn", dec_of[at], suf) * slopes
            enc = dots("gkn,nd->gkd", gate, xs[p])
            dec = dots("gkn,gnd->gkd", features, suf)
            if p:
                enc, dec = enc + sums["enc", at], dec + sums["dec", at]
            sums["enc", at], sums["dec", at] = enc, dec
    enc_new = sums["enc", 0] + from_other_core(sums["enc", 1])
    dec_new = sums["dec", 0] + from_other_core(sums["dec", 1])
    return (enc_new, dec_new)


def solution(mesh):
    in_specs = (P("feat", None), P("prefix", "feat", None), P("prefix", "feat", None))
    out_specs = (P("prefix", "feat", None), P("prefix", "feat", None))
    return jax.shard_map(
        step, mesh=mesh, in_specs=in_specs, out_specs=out_specs, check_vma=False
    )
```

```python
import functools

import jax
import jax.numpy as jnp
from jax import lax
from jax.experimental import pallas as pl
from jax.experimental.pallas import tpu as pltpu
from jax.sharding import PartitionSpec as P


F32 = jnp.float32
HIGH = lax.Precision.HIGH


def feat_index(y, x, core):
    return (y % 4) * 8 + (x % 4) * 2 + core


def from_chip(value, axis, step):
    dy, dx = (step, 0) if axis == 0 else (0, step)
    pairs = [
        (feat_index(y + dy, x + dx, c), feat_index(y, x, c))
        for y in range(4)
        for x in range(4)
        for c in range(2)
    ]
    return lax.ppermute(value, "feat", pairs)


def from_other_core(value):
    return lax.ppermute(value, "feat", [(f, f ^ 1) for f in range(32)])


def pack_kernel(*refs):
    out = refs[8]
    zs = out.shape[0]
    for k in range(2):
        for g in range(2):
            total = refs[4 * k][g]
            for r in refs[4 * k + 1 : 4 * k + 4]:
                total = total + r[g]
            own = total.shape[0] // zs
            at = (2 * g + k) * own
            for z in range(zs):
                out[z, at : at + own] = total[z * own : (z + 1) * own]


def unpack_kernel(back, a, b):
    zs = back.shape[0]
    own = a.shape[1] // zs
    for k, ref in enumerate((a, b)):
        for g in range(2):
            at = (2 * g + k) * own
            for z in range(zs):
                ref[g, z * own : (z + 1) * own] = back[z, at : at + own]


def suffix_kernel(factor, here, got, act, out):
    zs, rows, _ = got.shape
    half = rows // 2
    own = half // 2
    part = act.shape[0] // 2
    picked = []
    for k in range(2):
        a = act[k * part : k * part + own]
        for z in range(1, zs):
            at = k * part + z * own
            a = jnp.where(here[0] == z, act[at : at + own], a)
        picked.append(a)
    a = jnp.concatenate(picked, axis=0)
    errors = []
    total = None
    for z in range(zs):
        for g in range(2):
            d = got[z, g * half : (g + 1) * half]
            total = d if total is None else total + d
            errors.append(total - a)
    run = None
    for m in range(2 * zs - 1, -1, -1):
        run = errors[m] if run is None else run + errors[m]
        z, g = m // 2, m % 2
        out[z, g * half : (g + 1) * half] = factor * run


def shape(*dims, dtype=F32):
    return jax.ShapeDtypeStruct(dims, dtype)


def flat_call(body, ins, outs):
    vmem = pl.BlockSpec(memory_space=pltpu.VMEM)
    return pl.pallas_call(
        body,
        in_specs=[vmem] * len(ins),
        out_specs=[vmem] * len(outs),
        out_shape=outs,
        compiler_params=pltpu.CompilerParams(vmem_limit_bytes=4 * 2**20),
    )(*ins)


def line_kernel(*refs):
    out = refs[4]
    for i, r in enumerate(refs[:4]):
        rows = r.shape[1]
        out[:, i * rows : (i + 1) * rows] = r[...]


def join_kernel(eo, ep, do, dp, ea, da):
    half = eo.shape[1]
    for own, other, both in ((eo, ep, ea), (do, dp, da)):
        both[0, :half] = own[0]
        both[0, half:] = other[0]


def join(enc_own, enc_other, dec_own, dec_other):
    groups, feats, width = enc_own.shape
    part = pl.BlockSpec((1, feats, width), lambda g: (g, 0, 0))
    both = pl.BlockSpec((1, 2 * feats, width), lambda g: (g, 0, 0))
    return pl.pallas_call(
        join_kernel,
        name="join",
        grid=(groups,),
        in_specs=[part] * 4,
        out_specs=[both] * 2,
        out_shape=[shape(groups, 2 * feats, width)] * 2,
        compiler_params=pltpu.CompilerParams(vmem_limit_bytes=24 * 2**20),
    )(enc_own, enc_other, dec_own, dec_other)


def step(activations, enc_weight, dec_weight):
    rows, width = activations.shape
    groups, feats, _ = enc_weight.shape
    tokens = rows * lax.axis_size("feat")
    zs = lax.axis_size("prefix")
    factor = 2.0 / tokens
    part = rows // 2
    own = part // zs
    n = 4 * part
    dots = functools.partial(jnp.einsum, precision=HIGH)
    acts = [activations[:part], activations[part:]]
    halves = range(2)

    lines = []
    for k in halves:
        got = [acts[k]] + [from_chip(acts[k], k, e) for e in (1, 2, 3)]
        lines.append(jnp.concatenate(got, axis=0))
    x = {(0, k): lines[k] for k in halves}
    for e in (1, 3, 2):
        for k in halves:
            x[e, k] = from_chip(lines[k], 1 - k, e)

    enc_other, dec_other = from_other_core(enc_weight), from_other_core(dec_weight)
    enc_all, dec_all = join(enc_weight, enc_other, dec_weight, dec_other)
    dec_of = (dec_weight, dec_other)
    keys = [[(1, 0), (3, 0), (1, 1), (3, 1)], [(2, 0), (2, 1), (0, 0), (0, 1)]]
    last_keys = [keys[0][:2] + keys[1][2:], keys[0][2:] + keys[1][:2]]
    feat_p, made, xs = [], {}, []
    for p in range(2):
        xs.append(jnp.concatenate([x[key] for key in keys[p]], axis=0))
        pre = dots("gkd,nd->gkn", enc_all, xs[p])
        feat_p.append(jax.nn.softplus(4.0 * pre) / 4.0)
        if p == 0:
            out = dots("gkn,gkd->gnd", feat_p[p], dec_all)
            for i, key in enumerate(keys[p]):
                made[key] = out[:, i * n : (i + 1) * n]
            continue
        far = dots("gkn,gkd->gnd", feat_p[p][:, :, : 2 * n], dec_all)
        near = dots("gkn,gkd->gnd", feat_p[p][:, :, 2 * n :], dec_all)
        for k in halves:
            made[2, k] = far[:, k * n : (k + 1) * n]
            made[0, k] = near[:, k * n : (k + 1) * n]

    moved = {}
    for e in (1, 3, 2):
        for k in halves:
            moved[e, k] = from_chip(made[e, k], 1 - k, (-e) % 4)
    terms = []
    for k in halves:
        line = made[0, k] + moved[1, k] + moved[3, k]
        line = lax.optimization_barrier(line) + moved[2, k]
        line = line.reshape(groups, 4, part, width)
        terms.append(line[:, 0])
        for e in (1, 3, 2):
            terms.append(from_chip(line[:, e], k, (-e) % 4))
    (sent,) = flat_call(pack_kernel, terms, [shape(zs, 4 * own, width)])
    here = lax.axis_index("prefix").reshape(1)
    sent, here = lax.optimization_barrier((sent, here))
    got = lax.all_to_all(sent, "prefix", 0, 0)
    vmem = pl.BlockSpec(memory_space=pltpu.VMEM)
    suffix = pl.pallas_call(
        functools.partial(suffix_kernel, factor),
        name="suffix",
        in_specs=[pl.BlockSpec(memory_space=pltpu.SMEM), vmem, vmem],
        out_specs=vmem,
        out_shape=shape(zs, 4 * own, width),
        compiler_params=pltpu.CompilerParams(vmem_limit_bytes=4 * 2**20),
    )(here, got, activations)
    back = lax.all_to_all(suffix, "prefix", 0, 0)
    mine = flat_call(unpack_kernel, (back,), [shape(groups, part, width)] * 2)

    s = {}
    for k in halves:
        got = [mine[k]] + [from_chip(mine[k], k, e) for e in (1, 2, 3)]
        (s[0, k],) = flat_call(line_kernel, got, [shape(groups, n, width)])
    for e in (1, 3, 2):
        for k in halves:
            s[e, k] = from_chip(s[0, k], 1 - k, e)

    sums = {}
    for p in range(2):
        suf = jnp.concatenate([s[key] for key in last_keys[p]], axis=1)
        rows_p = jnp.concatenate([x[key] for key in last_keys[p]], axis=0)
        cut = 2 * n
        feat_of = (
            (feat_p[0][:, :, :cut], feat_p[1][:, :, cut:]),
            (feat_p[0][:, :, cut:], feat_p[1][:, :, :cut]),
        )
        feats_p = jnp.concatenate(feat_of[p], axis=2)
        for at in (1, 0):
            of = slice(at * feats, (at + 1) * feats)
            features = feats_p[:, of]
            slopes = -jnp.expm1(-4.0 * features)
            gate = dots("gkd,gnd->gkn", dec_of[at], suf) * slopes
            enc = dots("gkn,nd->gkd", gate, rows_p)
            dec = dots("gkn,gnd->gkd", features, suf)
            if p:
                enc, dec = enc + sums["enc", at], dec + sums["dec", at]
            sums["enc", at], sums["dec", at] = enc, dec
    enc_new = sums["enc", 0] + from_other_core(sums["enc", 1])
    dec_new = sums["dec", 0] + from_other_core(sums["dec", 1])
    return (enc_new, dec_new)


def solution(mesh):
    in_specs = (P("feat", None), P("prefix", "feat", None), P("prefix", "feat", None))
    out_specs = (P("prefix", "feat", None), P("prefix", "feat", None))
    return jax.shard_map(
        step, mesh=mesh, in_specs=in_specs, out_specs=out_specs, check_vma=False
    )
```
